32 devices in a mesh: ctx: 8 (over z, x), tp: 4 (over y, core).
Axes of the slice: x: 2, y: 2, z: 4, core: 2. Of those that a mesh axis runs over, the one named last changes fastest.
Arguments:
- queries: bfloat16 [1024, 1024], P('ctx', 'tp'), may hold values from -6 to 6
- keys: bfloat16 [1024, 1024], P('ctx', 'tp'), may hold values from -6 to 6
- values: bfloat16 [1024, 1024], P('ctx', 'tp'), may hold values from -6 to 6
- utterance: int32 [1024], P('ctx'), may hold values from 0 to 5, never falling along the last dimension, each value on 1 to 768 neighbouring positions
- w_out: bfloat16 [1024, 1536], P('tp'), may hold values from -0.5 to 0.5
- cotangent: bfloat16 [1024, 1536], P('ctx', 'tp'), may hold values from -2.5 to 2.5
Outputs:
- output: bfloat16 [1024, 1536], P('ctx', 'tp')
- grad_queries: bfloat16 [1024, 1024], P('ctx', 'tp')
- grad_keys: bfloat16 [1024, 1024], P('ctx', 'tp')
- grad_values: bfloat16 [1024, 1024], P('ctx', 'tp')
The draws below stay inside these ranges and needn't reach their ends.
Inputs may be any that keep to these rules, and one draw needn't show every extreme that they name: `utterance`: utterance numbers never fall along the frames; each of the 6 utterances covers 1 to 768 frames, and one covers exactly 768.
All inputs are finite; a program needn't handle non-finite values.
Results may differ from the reference program's by a relative error of at most 0.034.
Values may be sent and summed in bfloat16 or wider, within the bound.
A program may use at most 64 MiB of HBM per device.

```python
import math
import jax
import jax.numpy as jnp
import numpy as np
from jax import lax

D = 1536
HEADS = 16
HS = 64
FR = 128
UTTS = 6
FRAMES = 1024
MOST = 768


def paired_draw(key):
    column_count = HEADS * HS
    first_key, second_key = jax.random.split(key, 2)
    queries = jnp.clip(1.58 * jax.random.normal(first_key, (FRAMES, column_count), jnp.float32), -6.0, 6.0)
    keys = jnp.clip(1.58 * jax.random.normal(second_key, (FRAMES, column_count), jnp.float32), -6.0, 6.0)
    return (queries, keys)


def draw_queries(key, part):
    return paired_draw(key)[0].astype(jnp.bfloat16)


def draw_keys(key, part):
    return paired_draw(key)[1].astype(jnp.bfloat16)


def block_levels(stream_key, extent, pieces, low, high):
    level = 1.0
    for position, shards_of in pieces:
        draws = jax.random.uniform(jax.random.fold_in(jax.random.fold_in(stream_key, 6), position), (shards_of,), jnp.float32, low / len(pieces), high / len(pieces))
        level = level * jnp.repeat(jnp.exp(draws), extent[position] // shards_of).reshape((-1,) + (1,) * (len(extent) - 1 - position))
    return level


def length_profile(amount, total, bound, slope):
    loads = [(1 << 20) // math.isqrt(rank ** slope) + 1 for rank in range(2, amount + 1)]
    surplus, counts = total - bound - (amount - 1), [1] * (amount - 1)
    while surplus > 0:
        candidates = [i for i in range(amount - 1) if counts[i] < bound]
        whole, remaining = sum([loads[i] for i in candidates]), surplus
        for i in candidates:
            extra = min(bound - counts[i], max(1, remaining * loads[i] // whole), surplus)
            counts[i] = counts[i] + extra
            surplus = surplus - extra
    return np.array([bound] + counts)


def ragged(stream_key, number_of, total, most, lean):
    if number_of == 2:
        one = jax.random.randint(stream_key, (), max(1, total - most), min(most, total - 1) + 1)
        return jnp.stack([one, total - one])
    sizes = jnp.asarray(length_profile(number_of, total, most, lean), jnp.int32)
    pairs = (number_of - 1) // 2
    source_of, receiver = sizes[1:1 + 2 * pairs:2], sizes[2:2 + 2 * pairs:2]
    slack = jnp.minimum(source_of - 1, most - receiver)
    shifted = jax.random.randint(jax.random.fold_in(stream_key, 1), (pairs,), 0, 1 << 20) % (slack + 1)
    sizes = sizes.at[1:1 + 2 * pairs:2].set(source_of - shifted).at[2:2 + 2 * pairs:2].set(receiver + shifted)
    return sizes[jax.random.permutation(jax.random.fold_in(stream_key, 2), number_of)]


def scatter_about(rng, extent, scale, reach, pieces=(), held_as=jnp.bfloat16):
    array = jax.random.normal(rng, extent, jnp.float32) * scale
    if len(pieces) > 0:
        array = block_levels(rng, extent, pieces, -0.22, 0.18) * array
    return jnp.clip(array, min=-reach, max=reach).astype(held_as)


def setup_inputs(seed: int = 0) -> dict:
    key_list = jax.random.split(jax.random.key(seed), 7)
    return {
        "queries": draw_queries(jax.random.fold_in(key_list[6], 71), 0),
        "keys": draw_keys(jax.random.fold_in(key_list[6], 71), 0),
        "values": scatter_about(key_list[2], (FRAMES, HEADS * HS), 1.0, 6.0, ((0, 8), (1, 4))),
        "utterance": jnp.searchsorted(jnp.cumsum(ragged(key_list[3], UTTS, FRAMES, MOST, 2)), jnp.arange(FRAMES), side="right").astype(jnp.int32),
        "w_out": scatter_about(key_list[4], (HEADS * HS, D), (HEADS * HS // 8) ** -0.5, 0.5, ((0, 4),)),
        "cotangent": scatter_about(key_list[5], (FRAMES, D), 0.25, 2.5, ((0, 8), (1, 4))),
    }


def head_major(matrix):
    return matrix.reshape(matrix.shape[0], HEADS, HS).transpose(1, 0, 2)


def frame_major(stacked):
    return stacked.transpose(1, 0, 2).reshape(stacked.shape[1], HEADS * HS)


def split_pair(values32):
    upper_part = values32.astype(jnp.bfloat16)
    widened = lax.optimization_barrier(upper_part).astype(jnp.float32)
    return upper_part, (values32 - widened).astype(jnp.bfloat16)


def reference(queries, keys, values, utterance, w_out, cotangent):
    inv_root = HS ** -0.5
    blocks = FRAMES // FR
    query_heads = head_major(queries)
    key_heads = head_major(keys)
    value_heads = head_major(values)
    block_ids = utterance.reshape(blocks, FR)

    def forward_head(operands):
        query_one, key_one, value_one = operands

        def forward_block(inputs):
            query_block, ids_block = inputs
            scores = jnp.dot(query_block, key_one.T, preferred_element_type=jnp.float32) * inv_root
            same_utt = ids_block[:, None] == utterance[None, :]
            masked = jnp.where(same_utt, scores, -1e30)
            row_top = jnp.max(masked, axis=1, keepdims=True)
            weights = jnp.exp(masked - row_top)
            totals = jnp.sum(weights, axis=1, keepdims=True)
            mixture = jnp.dot(weights.astype(jnp.bfloat16), value_one, preferred_element_type=jnp.float32) / totals
            return mixture.astype(jnp.bfloat16), (row_top + jnp.log(totals))[:, 0]

        mixture, log_totals = lax.map(forward_block, (query_one.reshape(blocks, FR, HS), block_ids))
        return mixture.reshape(FRAMES, HS), log_totals.reshape(FRAMES)

    attn_heads, log_totals = lax.map(forward_head, (query_heads, key_heads, value_heads))
    attn = frame_major(attn_heads)
    output = jnp.dot(attn, w_out, preferred_element_type=jnp.float32).astype(jnp.bfloat16)
    attn_grad = jnp.dot(cotangent, w_out.T, preferred_element_type=jnp.float32).astype(jnp.bfloat16)
    grad_heads = head_major(attn_grad)
    delta = jnp.sum(grad_heads.astype(jnp.float32) * attn_heads.astype(jnp.float32), axis=2)
    lse_upper, lse_lower = split_pair(log_totals)
    delta_upper, delta_lower = split_pair(delta)
    lse_used = lse_upper.astype(jnp.float32) + lse_lower.astype(jnp.float32)
    delta_used = delta_upper.astype(jnp.float32) + delta_lower.astype(jnp.float32)

    def backward_head(operands):
        query_one, key_one, value_one, grad_one, lse_one, delta_one = operands

        def backward_block(running, inputs):
            key_total, value_total = running
            query_block, grad_block, lse_block, delta_block, ids_block = inputs
            scores = jnp.dot(query_block, key_one.T, preferred_element_type=jnp.float32) * inv_root
            same_utt = ids_block[:, None] == utterance[None, :]
            probability = jnp.exp(jnp.where(same_utt, scores - lse_block[:, None], -1e30))
            value_total = value_total + jnp.dot(probability.astype(jnp.bfloat16).T, grad_block, preferred_element_type=jnp.float32)
            dprobs = jnp.dot(grad_block, value_one.T, preferred_element_type=jnp.float32)
            dscores = (probability * (dprobs - delta_block[:, None])).astype(jnp.bfloat16)
            key_total = key_total + jnp.dot(dscores.T, query_block, preferred_element_type=jnp.float32)
            query_grad = jnp.dot(dscores, key_one, preferred_element_type=jnp.float32) * inv_root
            return (key_total, value_total), query_grad.astype(jnp.bfloat16)

        empty_sum = jnp.zeros((FRAMES, HS), jnp.float32)
        inputs = (query_one.reshape(blocks, FR, HS), grad_one.reshape(blocks, FR, HS),
                  lse_one.reshape(blocks, FR), delta_one.reshape(blocks, FR), block_ids)
        totals_pair, query_grad = lax.scan(backward_block, (empty_sum, empty_sum), inputs)
        key_total, value_total = totals_pair
        return (query_grad.reshape(FRAMES, HS), (key_total * inv_root).astype(jnp.bfloat16),
                value_total.astype(jnp.bfloat16))

    query_grads, key_grads, value_grads = lax.map(
        backward_head, (query_heads, key_heads, value_heads, grad_heads, lse_used, delta_used))
    return output, frame_major(query_grads), frame_major(key_grads), frame_major(value_grads)
```

```python
import functools
import math

import jax
import jax.numpy as jnp
from jax import lax
from jax.experimental import pallas as pl
from jax.experimental.pallas import tpu as pltpu
from jax.sharding import PartitionSpec as P

HS = 64
SLOTS = 16
APART = 131072.0
MESH = pl.DeviceIdType.MESH
F32 = jnp.float32
BF16 = jnp.bfloat16


def loop(low, high, body, carry):
    if high - low <= 1:
        for i in range(low, high):
            carry = body(i, carry)
        return carry
    return lax.fori_loop(low, high, body, carry)


def dot_nn(a, b):
    return jnp.dot(a, b, preferred_element_type=F32)


def dot_nt(a, b):
    return lax.dot_general(a, b, (((1,), (1,)), ((), ())), preferred_element_type=F32)


def turned(x):
    return jnp.transpose(x.astype(F32)).astype(BF16)


def remote(src, dst, send, recv, device):
    return pltpu.make_async_remote_copy(
        src_ref=src, dst_ref=dst, send_sem=send, recv_sem=recv, device_id=device, device_id_type=MESH
    )


def kernel(
    dims,
    q_in, k_in, v_in, u_ref, w_in, c_in,
    out_ref, dq_ref, dk_ref, dv_ref,
    q_v, k_v, v_v, w_v, cot,
    kv_snd, kv_all, kv_turn, q_snd, q_rcv, do_snd, do_rcv, o_snd, o_rcv, dq_snd, dq_rcv,
    grid, own, part_snd, part_rcv, fin_snd, fin_rcv, rs_snd, rs_rcv,
    local_sem, kv_s, kv_r, q_s, q_r, do_s, do_r, o_s, o_r, dq_s, dq_r, fin_s, fin_r,
    row_s, row_r, part_s, part_r, cot_s, cot_r, rs_s, rs_r,
):
    H, G, T, F = dims
    c = lax.axis_index("ctx")
    t = lax.axis_index("tp")
    h = c // G
    g = lax.rem(c, G)
    scale = HS ** (-0.5)
    expo = scale * math.log2(math.e)
    Q = H * F
    R = F * (2 if H % 2 == 0 else 1)

    loads = [
        pltpu.make_async_copy(src, dst, local_sem.at[i])
        for i, (src, dst) in enumerate(
            ((k_in, k_v), (v_in, v_v), (q_in, q_v), (c_in, cot.at[t]), (w_in, w_v))
        )
    ]
    for one in loads:
        one.start()

    def up(d):
        return lax.rem(h + d, H)

    def side(e):
        return lax.rem(g + e, G)

    def lane(f):
        return lax.rem(t + f, T)

    barrier = pltpu.get_barrier_semaphore()

    def greet(device):
        pl.semaphore_signal(barrier, inc=1, device_id=device, device_id_type=MESH)

    for d in range(1, H):
        greet((up(d) * G + g, t))

    def greet_side(e, carry):
        greet((h * G + side(e), t))
        return carry

    loop(1, G, greet_side, 0)
    for f in range(1, T):
        greet((c, lane(f)))

    same = (lax.broadcasted_iota(jnp.int32, (SLOTS, F), 0) == u_ref[...]).astype(F32).astype(BF16)
    loads[0].wait()
    loads[1].wait()
    keys, values = k_v[...], v_v[...]
    for i in range(H):
        cols = slice(i * HS, (i + 1) * HS)
        kv_snd[i, 0:F, :] = jnp.concatenate([keys[:, cols], values[:, cols]], axis=1)
        kv_snd[i, F:, :] = same
    loads[2].wait()
    q_turn = turned(q_v[...])
    for i in range(H):
        q_snd[i] = q_turn[i * HS:(i + 1) * HS, :]
    loads[3].wait()
    pl.semaphore_wait(barrier, (H - 1) + (G - 1) + (T - 1))

    def kv_copy(to, at):
        return remote(kv_snd.at[to], kv_all.at[g, at], kv_s.at[to], kv_r.at[at], (to * G + g, t))

    def column(snd, rcv, send, recv):
        def build(to, at):
            return remote(snd.at[to], rcv.at[at], send.at[to], recv.at[at], (to * G + g, t))
        return build

    q_copy = column(q_snd, q_rcv, q_s, q_r)
    do_copy = column(do_snd, do_rcv, do_s, do_r)
    o_copy = column(o_snd, o_rcv, o_s, o_r)
    dq_copy = column(dq_snd, dq_rcv, dq_s, dq_r)
    fin_copy = column(fin_snd, fin_rcv, fin_s, fin_r)

    def row_copy(to, at, block):
        return remote(
            kv_all.at[at, block], kv_all.at[at, block], row_s.at[to, block], row_r.at[at, block],
            (h * G + to, t),
        )

    def part_copy(to, at):
        return remote(part_snd.at[to], part_rcv.at[at], part_s.at[to], part_r.at[at], (h * G + to, t))

    def cot_copy(to, at):
        return remote(cot.at[at], cot.at[at], cot_s.at[to], cot_r.at[at], (c, to))

    def rs_copy(to, at):
        return remote(rs_snd.at[to], rs_rcv.at[at], rs_s.at[to], rs_r.at[at], (c, to))

    def send_column(build):
        for d in range(1, H):
            build(up(d), h).start()

    def wait_column(build):
        for d in range(1, H):
            build(up(d), up(d)).wait_recv()

    def sent_column(build):
        for d in range(1, H):
            build(up(d), h).wait_send()

    for d in range(1, H):
        kv_copy(up(d), h).start()
        q_copy(up(d), h).start()
    for f in range(1, T):
        cot_copy(lane(f), t).start()
    kv_all[g, h] = kv_snd[h]
    q_rcv[h] = q_snd[h]

    def forward(block):
        def step(e, carry):
            row_copy(side(e), g, block).start()
            return carry
        loop(1, G, step, 0)

    forward(h)
    for d in range(1, H):
        kv_copy(up(d), up(d)).wait_recv()
        forward(up(d))

    loads[4].wait()
    for f in range(1, T):
        cot_copy(lane(f), lane(f)).wait_recv()
    width = cot.shape[2]
    grad = dot_nt(w_v[:, 0:width], cot[0])
    for i in range(1, T):
        grad += dot_nt(w_v[:, i * width:(i + 1) * width], cot[i])
    grad = grad.astype(BF16)
    for i in range(H):
        do_snd[i] = grad[i * HS:(i + 1) * HS, :]
    send_column(do_copy)
    do_rcv[h] = do_snd[h]

    wait_column(q_copy)
    q_all = jnp.concatenate([q_rcv[i] for i in range(H)], axis=1)

    def away(i):
        hot = kv_all[g, i, F:, :].astype(F32)
        return ((hot - 1.0) * APART).astype(BF16)

    q_wide = jnp.concatenate([q_all, jnp.concatenate([away(i) for i in range(H)], axis=1)], axis=0)

    def score(at, top):
        for i in range(H):
            block = kv_all[at, i, 0:F, :]
            kv_turn[at, :, i * F:(i + 1) * F] = turned(block)
            hot = turned(kv_all[at, i, F:, :])
            wide = jnp.concatenate([block[:, 0:HS], hot], axis=1)
            s = dot_nn(wide, q_wide)
            grid[at, i * F:(i + 1) * F, :] = s
            top = jnp.maximum(top, jnp.max(s, axis=0, keepdims=True))
        return top

    top = score(g, jnp.full((1, Q), -jnp.inf, F32))

    def score_side(e, top):
        at = side(e)
        for i in range(H):
            row_copy(at, at, i).wait_recv()
        return score(at, top)

    top = loop(1, G, score_side, top)

    def mix(at, carry):
        total, mixed = carry
        for r in range(0, Q, R):
            w = jnp.exp2((grid[at, r:r + R, :] - top) * expo)
            grid[at, r:r + R, :] = w
            total = total + jnp.sum(w, axis=0, keepdims=True)
            mixed = mixed + dot_nn(kv_turn[at, HS:, r:r + R], w.astype(BF16))
        return total, mixed

    total, mixed = loop(0, G, mix, (jnp.zeros((1, Q), F32), jnp.zeros((HS, Q), F32)))
    inverse = 1.0 / total
    attn = (mixed * inverse).astype(BF16)
    for i in range(H):
        o_snd[i] = attn[:, i * F:(i + 1) * F]
    send_column(o_copy)
    o_rcv[h] = o_snd[h]

    wait_column(do_copy)
    do_all = jnp.concatenate([do_rcv[i] for i in range(H)], axis=1)
    delta = jnp.sum(do_all.astype(F32) * attn.astype(F32), axis=0, keepdims=True)

    def back(at, r):
        p = grid[at, r:r + R, :] * inverse
        dv = dot_nt(p.astype(BF16), do_all)
        rows = [kv_all[at, i, 0:F, HS:] for i in range(r // F, (r + R) // F)]
        dp = dot_nn(jnp.concatenate(rows, axis=0), do_all)
        ds = (p * (dp - delta)).astype(BF16)
        dk = dot_nt(ds, q_all) * scale
        dq = dot_nn(kv_turn[at, 0:HS, r:r + R], ds)
        return jnp.concatenate([dk, dv], axis=1), dq

    def back_side(e, query_total):
        at = side(e)
        for r in range(0, Q, R):
            part, dq = back(at, r)
            part_snd[at, r:r + R, :] = part.astype(BF16)
            query_total = query_total + dq
        part_copy(at, g).start()
        return query_total

    query_total = loop(1, G, back_side, jnp.zeros((HS, Q), F32))

    wait_column(o_copy)
    mine = turned(jnp.concatenate([o_rcv[i] for i in range(H)], axis=0))
    for i in range(T):
        rs_snd[i] = dot_nn(mine, w_v[:, i * width:(i + 1) * width]).astype(BF16)
    for f in range(1, T):
        rs_copy(lane(f), t).start()
    rs_rcv[t] = rs_snd[t]

    for r in range(0, Q, R):
        part, dq = back(g, r)
        own[r:r + R, :] = part
        query_total = query_total + dq
    query_out = (query_total * scale).astype(BF16)
    for i in range(H):
        dq_snd[i] = query_out[:, i * F:(i + 1) * F]
    send_column(dq_copy)
    dq_rcv[h] = dq_snd[h]

    def gather_part(e, carry):
        at = side(e)
        part_copy(at, at).wait_recv()
        own[...] += part_rcv[at].astype(F32)
        return carry

    loop(1, G, gather_part, 0)
    for i in range(H):
        fin_snd[i] = own[i * F:(i + 1) * F, :].astype(BF16)
    send_column(fin_copy)
    fin_rcv[h] = fin_snd[h]

    for f in range(1, T):
        rs_copy(lane(f), lane(f)).wait_recv()
    summed = rs_rcv[0].astype(F32)
    for i in range(1, T):
        summed += rs_rcv[i].astype(F32)
    out_ref[...] = summed.astype(BF16)

    wait_column(dq_copy)
    dq_ref[...] = turned(jnp.concatenate([dq_rcv[i] for i in range(H)], axis=0))
    wait_column(fin_copy)
    dk_ref[...] = jnp.concatenate([fin_rcv[i, :, 0:HS] for i in range(H)], axis=1)
    dv_ref[...] = jnp.concatenate([fin_rcv[i, :, HS:] for i in range(H)], axis=1)

    for build in (kv_copy, q_copy, do_copy, o_copy, dq_copy, fin_copy):
        sent_column(build)

    def sent_side(e, carry):
        for i in range(H):
            row_copy(side(e), g, i).wait_send()
        part_copy(side(e), g).wait_send()
        return carry

    loop(1, G, sent_side, 0)
    for f in range(1, T):
        cot_copy(lane(f), t).wait_send()
        rs_copy(lane(f), t).wait_send()


def solution(mesh):
    n, T = mesh.shape["ctx"], mesh.shape["tp"]

    def step(queries, keys, values, utterance, w_out, cotangent):
        F, columns = queries.shape
        H = columns // HS
        G = n // H
        D = w_out.shape[1]
        width = cotangent.shape[1]
        Q = H * F
        vm = pltpu.VMEM
        dma = pltpu.SemaphoreType.DMA
        shapes = [
            vm((F, columns), BF16), vm((F, columns), BF16), vm((F, columns), BF16), vm((columns, D), BF16),
            vm((T, F, width), BF16),
            vm((H, F + SLOTS, 2 * HS), BF16), vm((G, H, F + SLOTS, 2 * HS), BF16), vm((G, 2 * HS, Q), BF16),
            vm((H, HS, F), BF16), vm((H, HS, F), BF16), vm((H, HS, F), BF16), vm((H, HS, F), BF16),
            vm((H, HS, F), BF16), vm((H, HS, F), BF16), vm((H, HS, F), BF16), vm((H, HS, F), BF16),
            vm((G, Q, Q), F32), vm((Q, 2 * HS), F32),
            vm((G, Q, 2 * HS), BF16), vm((G, Q, 2 * HS), BF16),
            vm((H, F, 2 * HS), BF16), vm((H, F, 2 * HS), BF16),
            vm((T, F, width), BF16), vm((T, F, width), BF16),
            dma((5,)),
        ] + [dma((H,))] * 12 + [dma((G, H))] * 2 + [dma((G,))] * 2 + [dma((T,))] * 4
        whole = pl.BlockSpec(memory_space=pl.ANY)
        here = pl.BlockSpec(memory_space=pltpu.VMEM)
        return pl.pallas_call(
            functools.partial(kernel, (H, G, T, F)),
            out_shape=(
                jax.ShapeDtypeStruct((F, width), BF16),
                jax.ShapeDtypeStruct((F, columns), BF16),
                jax.ShapeDtypeStruct((F, columns), BF16),
                jax.ShapeDtypeStruct((F, columns), BF16),
            ),
            in_specs=[whole, whole, whole, here, whole, whole],
            out_specs=(here, here, here, here),
            scratch_shapes=shapes,
            compiler_params=pltpu.CompilerParams(
                collective_id=0, has_side_effects=True, vmem_limit_bytes=48 * 1024 * 1024
            ),
        )(queries, keys, values, utterance.reshape(1, F), w_out, cotangent)

    placed = (P("ctx", "tp"), P("ctx", "tp"), P("ctx", "tp"), P("ctx"), P("tp", None), P("ctx", "tp"))
    return jax.shard_map(
        step, mesh=mesh, in_specs=placed, out_specs=(P("ctx", "tp"),) * 4, check_vma=False
    )
```

```python
import functools
import math

import jax
import jax.numpy as jnp
from jax import lax
from jax.experimental import pallas as pl
from jax.experimental.pallas import tpu as pltpu
from jax.sharding import PartitionSpec as P

HS = 64
SLOTS = 16
APART = 131072.0
MESH = pl.DeviceIdType.MESH
F32 = jnp.float32
BF16 = jnp.bfloat16


def loop(low, high, body, carry):
    if high - low <= 1:
        for i in range(low, high):
            carry = body(i, carry)
        return carry
    return lax.fori_loop(low, high, body, carry)


def pairs(items):
    items = list(items)
    step = 2 if len(items) % 2 == 0 else 1
    return [items[i:i + step] for i in range(0, len(items), step)]


def dot_nn(a, b):
    return jnp.dot(a, b, preferred_element_type=F32)


def dot_nt(a, b):
    return lax.dot_general(a, b, (((1,), (1,)), ((), ())), preferred_element_type=F32)


def turned(x):
    return jnp.transpose(x.astype(F32)).astype(BF16)


def remote(src, dst, send, recv, device):
    return pltpu.make_async_remote_copy(
        src_ref=src, dst_ref=dst, send_sem=send, recv_sem=recv, device_id=device, device_id_type=MESH
    )


def kernel(
    dims,
    q_in, k_in, v_in, u_ref, w_in, c_in,
    out_ref, dq_ref, dk_ref, dv_ref,
    q_v, k_v, v_v, w_v, cot,
    kv_snd, kv_all, kv_turn, q_snd, q_rcv, do_snd, do_rcv, o_snd, o_rcv, dq_snd, dq_rcv,
    grid, tops, part_snd, part_rcv, fin_snd, fin_rcv, rs_snd, rs_rcv,
    local_sem, kv_s, kv_r, q_s, q_r, do_s, do_r, o_s, o_r, dq_s, dq_r, fin_s, fin_r,
    row_s, row_r, part_s, part_r, cot_s, cot_r, rs_s, rs_r,
):
    H, G, T, F = dims
    c = lax.axis_index("ctx")
    t = lax.axis_index("tp")
    h = c // G
    g = lax.rem(c, G)
    scale = HS ** (-0.5)
    expo = scale * math.log2(math.e)
    Q = H * F

    def up(d):
        return lax.rem(h + d, H)

    def side(e):
        return lax.rem(g + e, G)

    def lane(f):
        return lax.rem(t + f, T)

    barrier = pltpu.get_barrier_semaphore()

    def greet(device):
        pl.semaphore_signal(barrier, inc=1, device_id=device, device_id_type=MESH)

    for d in range(1, H):
        greet((up(d) * G + g, t))

    def greet_side(e, carry):
        greet((h * G + side(e), t))
        return carry

    loop(1, G, greet_side, 0)
    for f in range(1, T):
        greet((c, lane(f)))

    loads = [
        pltpu.make_async_copy(src, dst, local_sem.at[i])
        for i, (src, dst) in enumerate(
            ((k_in, k_v), (v_in, v_v), (q_in, q_v), (c_in, cot.at[t]), (w_in, w_v))
        )
    ]
    for one in loads:
        one.start()

    same = (lax.broadcasted_iota(jnp.int32, (SLOTS, F), 0) == u_ref[...]).astype(F32).astype(BF16)
    loads[0].wait()
    loads[1].wait()
    keys, values = k_v[...], v_v[...]
    for i in range(H):
        cols = slice(i * HS, (i + 1) * HS)
        kv_snd[i, 0:F, :] = jnp.concatenate([keys[:, cols], values[:, cols]], axis=1)
        kv_snd[i, F:, :] = same
    loads[2].wait()
    q_turn = turned(q_v[...])
    for i in range(H):
        q_snd[i] = q_turn[i * HS:(i + 1) * HS, :]
    loads[3].wait()
    pl.semaphore_wait(barrier, (H - 1) + (G - 1) + (T - 1))

    def kv_copy(to, at):
        return remote(kv_snd.at[to], kv_all.at[g, at], kv_s.at[to], kv_r.at[at], (to * G + g, t))

    def column(snd, rcv, send, recv):
        def build(to, at):
            return remote(snd.at[to], rcv.at[at], send.at[to], recv.at[at], (to * G + g, t))
        return build

    q_copy = column(q_snd, q_rcv, q_s, q_r)
    do_copy = column(do_snd, do_rcv, do_s, do_r)
    o_copy = column(o_snd, o_rcv, o_s, o_r)
    dq_copy = column(dq_snd, dq_rcv, dq_s, dq_r)
    fin_copy = column(fin_snd, fin_rcv, fin_s, fin_r)

    def row_copy(to, at, block):
        return remote(
            kv_all.at[at, block], kv_all.at[at, block], row_s.at[to, block], row_r.at[at, block],
            (h * G + to, t),
        )

    def part_copy(to, at, block):
        return remote(
            part_snd.at[to, block], part_rcv.at[at, block], part_s.at[to, block], part_r.at[at, block],
            (h * G + to, t),
        )

    def cot_copy(to, at):
        return remote(cot.at[at], cot.at[at], cot_s.at[to], cot_r.at[at], (c, to))

    def rs_copy(to, at):
        return remote(rs_snd.at[to], rs_rcv.at[at], rs_s.at[to], rs_r.at[at], (c, to))

    def send_column(build):
        for d in range(1, H):
            build(up(d), h).start()

    def wait_column(build):
        for d in range(H - 1, 0, -1):
            build(up(d), up(d)).wait_recv()

    def sent_column(build):
        for d in range(1, H):
            build(up(d), h).wait_send()

    for d in range(1, H):
        kv_copy(up(d), h).start()
        q_copy(up(d), h).start()
    for f in range(1, T):
        cot_copy(lane(f), t).start()
    kv_all[g, h] = kv_snd[h]
    q_rcv[h] = q_snd[h]

    def forward(block):
        def step(e, carry):
            row_copy(side(e), g, block).start()
            return carry
        loop(1, G, step, 0)

    forward(h)
    for d in range(H - 1, 0, -1):
        kv_copy(up(d), up(d)).wait_recv()
        forward(up(d))

    loads[4].wait()
    for f in range(1, T):
        cot_copy(lane(f), lane(f)).wait_recv()
    width = cot.shape[2]
    grad = dot_nt(w_v[:, 0:width], cot[0])
    for i in range(1, T):
        grad += dot_nt(w_v[:, i * width:(i + 1) * width], cot[i])
    grad = grad.astype(BF16)
    for i in range(H):
        do_snd[i] = grad[i * HS:(i + 1) * HS, :]
    send_column(do_copy)
    do_rcv[h] = do_snd[h]

    wait_column(q_copy)
    q_all = jnp.concatenate([q_rcv[i] for i in range(H)], axis=1)

    def away(i):
        hot = kv_all[g, i, F:, :].astype(F32)
        return ((hot - 1.0) * APART).astype(BF16)

    q_wide = jnp.concatenate([q_all, jnp.concatenate([away(i) for i in range(H)], axis=1)], axis=0)

    def ahead(at):
        top = None
        for i in range(H):
            block = kv_all[at, i, 0:F, :]
            kv_turn[at, i] = turned(block)
            hot = turned(kv_all[at, i, F:, :])
            wide = jnp.concatenate([block[:, 0:HS], hot], axis=1)
            s = dot_nn(wide, q_wide)
            grid[at, i] = s
            here = jnp.max(s, axis=0, keepdims=True)
            top = here if top is None else jnp.maximum(top, here)
        tops[at] = top
        total, mixed = jnp.zeros((1, Q), F32), jnp.zeros((HS, Q), F32)
        for pair in pairs(range(H)):
            parts = []
            for i in pair:
                w = jnp.exp2((grid[at, i] - top) * expo)
                grid[at, i] = w
                total = total + jnp.sum(w, axis=0, keepdims=True)
                parts.append(w.astype(BF16))
            lanes = jnp.concatenate([kv_turn[at, i, HS:, :] for i in pair], axis=1)
            mixed = mixed + dot_nn(lanes, jnp.concatenate(parts, axis=0))
        return top, total, mixed

    def ahead_side(e, carry):
        top, total, mixed = carry
        at = side(e)
        for i in range(H):
            row_copy(at, at, i).wait_recv()
        new, more, other = ahead(at)
        both = jnp.maximum(top, new)
        old_part, new_part = jnp.exp2((top - both) * expo), jnp.exp2((new - both) * expo)
        return both, total * old_part + more * new_part, mixed * old_part + other * new_part

    top, total, mixed = loop(1, G, ahead_side, ahead(g))
    inverse = 1.0 / total
    attn = (mixed * inverse).astype(BF16)
    for i in range(H):
        o_snd[i] = attn[:, i * F:(i + 1) * F]
    send_column(o_copy)
    o_rcv[h] = o_snd[h]

    wait_column(do_copy)
    do_all = jnp.concatenate([do_rcv[i] for i in range(H)], axis=1)
    delta = jnp.sum(do_all.astype(F32) * attn.astype(F32), axis=0, keepdims=True)

    def back(at, pair):
        factor = jnp.exp2((tops[at] - top) * expo) * inverse
        p = jnp.concatenate([grid[at, b] for b in pair], axis=0) * factor
        dv = dot_nt(p.astype(BF16), do_all)
        rows = jnp.concatenate([kv_all[at, b, 0:F, HS:] for b in pair], axis=0)
        ds = (p * (dot_nn(rows, do_all) - delta)).astype(BF16)
        dk = dot_nt(ds, q_all) * scale
        dq = dot_nn(jnp.concatenate([kv_turn[at, b, 0:HS, :] for b in pair], axis=1), ds)
        return jnp.concatenate([dk, dv], axis=1), dq

    order = [up(d) for d in range(1, H)] + [h]

    def back_side(e, query_total):
        at = side(e)
        for pair in pairs(order):
            part, dq = back(at, pair)
            for i, b in enumerate(pair):
                part_snd[at, b] = part[i * F:(i + 1) * F, :].astype(BF16)
                part_copy(at, g, b).start()
            query_total = query_total + dq
        return query_total

    query_total = loop(1, G, back_side, jnp.zeros((HS, Q), F32))

    wait_column(o_copy)
    mine = turned(jnp.concatenate([o_rcv[i] for i in range(H)], axis=0))
    for i in range(T):
        rs_snd[i] = dot_nn(mine, w_v[:, i * width:(i + 1) * width]).astype(BF16)
    for f in range(1, T):
        rs_copy(lane(f), t).start()
    rs_rcv[t] = rs_snd[t]

    def finish(b, part):
        def gather(e, sofar):
            at = side(e)
            part_copy(at, at, b).wait_recv()
            return sofar + part_rcv[at, b].astype(F32)

        fin_snd[b] = loop(1, G, gather, part).astype(BF16)

    for number, pair in enumerate(pairs(order)):
        part, dq = back(g, pair)
        query_total = query_total + dq
        for i, b in enumerate(pair):
            finish(b, part[i * F:(i + 1) * F, :])
            if number * len(pair) + i < H - 1:
                fin_copy(b, h).start()
    fin_rcv[h] = fin_snd[h]
    query_out = (query_total * scale).astype(BF16)
    for i in range(H):
        dq_snd[i] = query_out[:, i * F:(i + 1) * F]
    send_column(dq_copy)
    dq_rcv[h] = dq_snd[h]

    for f in range(1, T):
        rs_copy(lane(f), lane(f)).wait_recv()
    summed = rs_rcv[0].astype(F32)
    for i in range(1, T):
        summed += rs_rcv[i].astype(F32)
    out_ref[...] = summed.astype(BF16)

    wait_column(dq_copy)
    dq_ref[...] = turned(jnp.concatenate([dq_rcv[i] for i in range(H)], axis=0))
    wait_column(fin_copy)
    dk_ref[...] = jnp.concatenate([fin_rcv[i, :, 0:HS] for i in range(H)], axis=1)
    dv_ref[...] = jnp.concatenate([fin_rcv[i, :, HS:] for i in range(H)], axis=1)

    for build in (kv_copy, q_copy, do_copy, o_copy, dq_copy, fin_copy):
        sent_column(build)

    def sent_side(e, carry):
        for i in range(H):
            row_copy(side(e), g, i).wait_send()
            part_copy(side(e), g, i).wait_send()
        return carry

    loop(1, G, sent_side, 0)
    for f in range(1, T):
        cot_copy(lane(f), t).wait_send()
        rs_copy(lane(f), t).wait_send()


def store(a, b, c, d, a_out, b_out, c_out, d_out, sem):
    moves = [
        pltpu.make_async_copy(src, dst, sem.at[i])
        for i, (src, dst) in enumerate(((a, a_out), (b, b_out), (c, c_out), (d, d_out)))
    ]
    for one in moves:
        one.start()
    for one in moves:
        one.wait()


def solution(mesh):
    n, T = mesh.shape["ctx"], mesh.shape["tp"]

    def step(queries, keys, values, utterance, w_out, cotangent):
        F, columns = queries.shape
        H = columns // HS
        G = n // H
        D = w_out.shape[1]
        width = cotangent.shape[1]
        Q = H * F
        vm = pltpu.VMEM
        dma = pltpu.SemaphoreType.DMA
        shapes = [
            vm((F, columns), BF16), vm((F, columns), BF16), vm((F, columns), BF16), vm((columns, D), BF16),
            vm((T, F, width), BF16),
            vm((H, F + SLOTS, 2 * HS), BF16), vm((G, H, F + SLOTS, 2 * HS), BF16), vm((G, H, 2 * HS, F), BF16),
            vm((H, HS, F), BF16), vm((H, HS, F), BF16), vm((H, HS, F), BF16), vm((H, HS, F), BF16),
            vm((H, HS, F), BF16), vm((H, HS, F), BF16), vm((H, HS, F), BF16), vm((H, HS, F), BF16),
            vm((G, H, F, Q), F32), vm((G, 1, Q), F32),
            vm((G, H, F, 2 * HS), BF16), vm((G, H, F, 2 * HS), BF16),
            vm((H, F, 2 * HS), BF16), vm((H, F, 2 * HS), BF16),
            vm((T, F, width), BF16), vm((T, F, width), BF16),
            dma((5,)),
        ] + [dma((H,))] * 12 + [dma((G, H))] * 4 + [dma((T,))] * 4
        whole = pl.BlockSpec(memory_space=pltpu.HBM)
        here = pl.BlockSpec(memory_space=pltpu.VMEM)
        made = pl.pallas_call(
            functools.partial(kernel, (H, G, T, F)),
            out_shape=(
                jax.ShapeDtypeStruct((F, width), BF16),
                jax.ShapeDtypeStruct((F, columns), BF16),
                jax.ShapeDtypeStruct((F, columns), BF16),
                jax.ShapeDtypeStruct((F, columns), BF16),
            ),
            in_specs=[whole, whole, whole, here, whole, whole],
            out_specs=(here, here, here, here),
            scratch_shapes=shapes,
            compiler_params=pltpu.CompilerParams(
                collective_id=0, has_side_effects=True, vmem_limit_bytes=62 * 1024 * 1024
            ),
        )(queries, keys, values, utterance.reshape(1, F), w_out, cotangent)
        return pl.pallas_call(
            store,
            out_shape=tuple(jax.ShapeDtypeStruct(x.shape, x.dtype) for x in made),
            in_specs=[whole] * 4,
            out_specs=(whole,) * 4,
            scratch_shapes=[dma((4,))],
        )(*made)

    placed = (P("ctx", "tp"), P("ctx", "tp"), P("ctx", "tp"), P("ctx"), P("tp", None), P("ctx", "tp"))
    return jax.shard_map(
        step, mesh=mesh, in_specs=placed, out_specs=(P("ctx", "tp"),) * 4, check_vma=False
    )
```

```python
import functools
import math

import jax
import jax.numpy as jnp
from jax import lax
from jax.experimental import pallas as pl
from jax.experimental.pallas import tpu as pltpu
from jax.sharding import PartitionSpec as P

HS = 64
SLOTS = 16
APART = 131072.0
MESH = pl.DeviceIdType.MESH
F32 = jnp.float32
BF16 = jnp.bfloat16


def loop(low, high, body, carry):
    if high - low <= 1:
        for i in range(low, high):
            carry = body(i, carry)
        return carry
    return lax.fori_loop(low, high, body, carry)


def pairs(items):
    items = list(items)
    step = 2 if len(items) % 2 == 0 else 1
    return [items[i:i + step] for i in range(0, len(items), step)]


def dot_nn(a, b):
    return jnp.dot(a, b, preferred_element_type=F32)


def dot_nt(a, b):
    return lax.dot_general(a, b, (((1,), (1,)), ((), ())), preferred_element_type=F32)


def turned(x):
    return jnp.transpose(x.astype(F32)).astype(BF16)


def remote(src, dst, send, recv, device):
    return pltpu.make_async_remote_copy(
        src_ref=src, dst_ref=dst, send_sem=send, recv_sem=recv, device_id=device, device_id_type=MESH
    )


def kernel(
    dims,
    q_in, k_in, v_in, u_in, w_in, c_in,
    out_ref, dq_ref, dk_ref, dv_ref,
    q_v, k_v, v_v, u_v, w_v, cot,
    kv_snd, kv_all, kv_turn, q_snd, q_rcv, do_snd, do_rcv, o_snd, o_rcv, dq_snd, dq_rcv,
    grid, tops, part_snd, part_rcv, fin_snd, fin_rcv, rs_snd, rs_rcv,
    local_sem, kv_s, kv_r, q_s, q_r, do_s, do_r, o_s, o_r, dq_s, dq_r, fin_s, fin_r,
    row_s, row_r, part_s, part_r, cot_s, cot_r, rs_s, rs_r,
):
    H, G, T, F = dims
    c = lax.axis_index("ctx")
    t = lax.axis_index("tp")
    h = c // G
    g = lax.rem(c, G)
    scale = HS ** (-0.5)
    expo = scale * math.log2(math.e)
    Q = H * F

    def up(d):
        return lax.rem(h + d, H)

    def side(e):
        return lax.rem(g + e, G)

    def lane(f):
        return lax.rem(t + f, T)

    barrier = pltpu.get_barrier_semaphore()

    def greet(device):
        pl.semaphore_signal(barrier, inc=1, device_id=device, device_id_type=MESH)

    for d in range(1, H):
        greet((up(d) * G + g, t))

    def greet_side(e, carry):
        greet((h * G + side(e), t))
        return carry

    loop(1, G, greet_side, 0)
    for f in range(1, T):
        greet((c, lane(f)))

    loads = [
        pltpu.make_async_copy(src, dst, local_sem.at[i])
        for i, (src, dst) in enumerate(
            ((k_in, k_v), (v_in, v_v), (q_in, q_v), (c_in, cot.at[t]), (w_in, w_v), (u_in, u_v))
        )
    ]
    for one in loads:
        one.start()

    loads[5].wait()
    same = (lax.broadcasted_iota(jnp.int32, (SLOTS, F), 0) == u_v[...]).astype(F32).astype(BF16)
    loads[0].wait()
    loads[1].wait()
    keys, values = k_v[...], v_v[...]
    for i in range(H):
        cols = slice(i * HS, (i + 1) * HS)
        kv_snd[i, 0:F, :] = jnp.concatenate([keys[:, cols], values[:, cols]], axis=1)
        kv_snd[i, F:, :] = same
    loads[2].wait()
    q_turn = turned(q_v[...])
    for i in range(H):
        q_snd[i] = q_turn[i * HS:(i + 1) * HS, :]
    loads[3].wait()
    pl.semaphore_wait(barrier, (H - 1) + (G - 1) + (T - 1))

    def kv_copy(to, at):
        return remote(kv_snd.at[to], kv_all.at[g, at], kv_s.at[to], kv_r.at[at], (to * G + g, t))

    def column(snd, rcv, send, recv):
        def build(to, at):
            return remote(snd.at[to], rcv.at[at], send.at[to], recv.at[at], (to * G + g, t))
        return build

    q_copy = column(q_snd, q_rcv, q_s, q_r)
    do_copy = column(do_snd, do_rcv, do_s, do_r)
    o_copy = column(o_snd, o_rcv, o_s, o_r)
    dq_copy = column(dq_snd, dq_rcv, dq_s, dq_r)
    fin_copy = column(fin_snd, fin_rcv, fin_s, fin_r)

    def row_copy(to, at, block):
        return remote(
            kv_all.at[at, block], kv_all.at[at, block], row_s.at[to, block], row_r.at[at, block],
            (h * G + to, t),
        )

    def part_copy(to, at, block):
        return remote(
            part_snd.at[to, block], part_rcv.at[at, block], part_s.at[to, block], part_r.at[at, block],
            (h * G + to, t),
        )

    def cot_copy(to, at):
        return remote(cot.at[at], cot.at[at], cot_s.at[to], cot_r.at[at], (c, to))

    def rs_copy(to, at):
        return remote(rs_snd.at[to], rs_rcv.at[at], rs_s.at[to], rs_r.at[at], (c, to))

    def send_column(build):
        for d in range(1, H):
            build(up(d), h).start()

    def wait_column(build):
        for d in range(H - 1, 0, -1):
            build(up(d), up(d)).wait_recv()

    def sent_column(build):
        for d in range(1, H):
            build(up(d), h).wait_send()

    for d in range(1, H):
        kv_copy(up(d), h).start()
        q_copy(up(d), h).start()
    for f in range(1, T):
        cot_copy(lane(f), t).start()
    kv_all[g, h] = kv_snd[h]
    q_rcv[h] = q_snd[h]

    def forward(block):
        def step(e, carry):
            row_copy(side(e), g, block).start()
            return carry
        loop(1, G, step, 0)

    forward(h)
    for d in range(H - 1, 0, -1):
        kv_copy(up(d), up(d)).wait_recv()
        forward(up(d))

    loads[4].wait()
    for f in range(1, T):
        cot_copy(lane(f), lane(f)).wait_recv()
    width = cot.shape[2]
    grad = dot_nt(w_v[:, 0:width], cot[0])
    for i in range(1, T):
        grad += dot_nt(w_v[:, i * width:(i + 1) * width], cot[i])
    grad = grad.astype(BF16)
    for i in range(H):
        do_snd[i] = grad[i * HS:(i + 1) * HS, :]
    send_column(do_copy)
    do_rcv[h] = do_snd[h]

    wait_column(q_copy)
    q_all = jnp.concatenate([q_rcv[i] for i in range(H)], axis=1)

    def away(i):
        hot = kv_all[g, i, F:, :].astype(F32)
        return ((hot - 1.0) * APART).astype(BF16)

    q_wide = jnp.concatenate([q_all, jnp.concatenate([away(i) for i in range(H)], axis=1)], axis=0)

    def ahead(at):
        top = None
        for i in range(H):
            block = kv_all[at, i, 0:F, :]
            kv_turn[at, i] = turned(block)
            hot = turned(kv_all[at, i, F:, :])
            wide = jnp.concatenate([block[:, 0:HS], hot], axis=1)
            s = dot_nn(wide, q_wide)
            grid[at, i] = s
            here = jnp.max(s, axis=0, keepdims=True)
            top = here if top is None else jnp.maximum(top, here)
        tops[at] = top
        total, mixed = jnp.zeros((1, Q), F32), jnp.zeros((HS, Q), F32)
        for pair in pairs(range(H)):
            parts = []
            for i in pair:
                w = jnp.exp2((grid[at, i] - top) * expo)
                grid[at, i] = w
                total = total + jnp.sum(w, axis=0, keepdims=True)
                parts.append(w.astype(BF16))
            lanes = jnp.concatenate([kv_turn[at, i, HS:, :] for i in pair], axis=1)
            mixed = mixed + dot_nn(lanes, jnp.concatenate(parts, axis=0))
        return top, total, mixed

    def ahead_side(e, carry):
        top, total, mixed = carry
        at = side(e)
        for i in range(H):
            row_copy(at, at, i).wait_recv()
        new, more, other = ahead(at)
        both = jnp.maximum(top, new)
        old_part, new_part = jnp.exp2((top - both) * expo), jnp.exp2((new - both) * expo)
        return both, total * old_part + more * new_part, mixed * old_part + other * new_part

    top, total, mixed = loop(1, G, ahead_side, ahead(g))
    inverse = 1.0 / total
    attn = (mixed * inverse).astype(BF16)
    for i in range(H):
        o_snd[i] = attn[:, i * F:(i + 1) * F]
    send_column(o_copy)
    o_rcv[h] = o_snd[h]

    wait_column(do_copy)
    do_all = jnp.concatenate([do_rcv[i] for i in range(H)], axis=1)
    delta = jnp.sum(do_all.astype(F32) * attn.astype(F32), axis=0, keepdims=True)

    def back(at, pair):
        factor = jnp.exp2((tops[at] - top) * expo) * inverse
        p = jnp.concatenate([grid[at, b] for b in pair], axis=0) * factor
        dv = dot_nt(p.astype(BF16), do_all)
        rows = jnp.concatenate([kv_all[at, b, 0:F, HS:] for b in pair], axis=0)
        ds = (p * (dot_nn(rows, do_all) - delta)).astype(BF16)
        dk = dot_nt(ds, q_all) * scale
        dq = dot_nn(jnp.concatenate([kv_turn[at, b, 0:HS, :] for b in pair], axis=1), ds)
        return jnp.concatenate([dk, dv], axis=1), dq

    order = [up(d) for d in range(1, H)] + [h]

    def back_side(e, query_total):
        at = side(e)
        for pair in pairs(order):
            part, dq = back(at, pair)
            for i, b in enumerate(pair):
                part_snd[at, b] = part[i * F:(i + 1) * F, :].astype(BF16)
                part_copy(at, g, b).start()
            query_total = query_total + dq
        return query_total

    query_total = loop(1, G, back_side, jnp.zeros((HS, Q), F32))

    wait_column(o_copy)
    mine = turned(jnp.concatenate([o_rcv[i] for i in range(H)], axis=0))
    for i in range(T):
        rs_snd[i] = dot_nn(mine, w_v[:, i * width:(i + 1) * width]).astype(BF16)
    for f in range(1, T):
        rs_copy(lane(f), t).start()
    rs_rcv[t] = rs_snd[t]

    def finish(b, part):
        def gather(e, sofar):
            at = side(e)
            part_copy(at, at, b).wait_recv()
            return sofar + part_rcv[at, b].astype(F32)

        fin_snd[b] = loop(1, G, gather, part).astype(BF16)

    for number, pair in enumerate(pairs(order)):
        part, dq = back(g, pair)
        query_total = query_total + dq
        for i, b in enumerate(pair):
            finish(b, part[i * F:(i + 1) * F, :])
            if number * len(pair) + i < H - 1:
                fin_copy(b, h).start()
    fin_rcv[h] = fin_snd[h]
    query_out = (query_total * scale).astype(BF16)
    for i in range(H):
        dq_snd[i] = query_out[:, i * F:(i + 1) * F]
    send_column(dq_copy)
    dq_rcv[h] = dq_snd[h]

    for f in range(1, T):
        rs_copy(lane(f), lane(f)).wait_recv()
    summed = rs_rcv[0].astype(F32)
    for i in range(1, T):
        summed += rs_rcv[i].astype(F32)
    out_ref[...] = summed.astype(BF16)

    wait_column(dq_copy)
    dq_ref[...] = turned(jnp.concatenate([dq_rcv[i] for i in range(H)], axis=0))
    wait_column(fin_copy)
    dk_ref[...] = jnp.concatenate([fin_rcv[i, :, 0:HS] for i in range(H)], axis=1)
    dv_ref[...] = jnp.concatenate([fin_rcv[i, :, HS:] for i in range(H)], axis=1)

    for build in (kv_copy, q_copy, do_copy, o_copy, dq_copy, fin_copy):
        sent_column(build)

    def sent_side(e, carry):
        for i in range(H):
            row_copy(side(e), g, i).wait_send()
            part_copy(side(e), g, i).wait_send()
        return carry

    loop(1, G, sent_side, 0)
    for f in range(1, T):
        cot_copy(lane(f), t).wait_send()
        rs_copy(lane(f), t).wait_send()


def store(a, b, c, d, a_out, b_out, c_out, d_out, sem):
    moves = [
        pltpu.make_async_copy(src, dst, sem.at[i])
        for i, (src, dst) in enumerate(((a, a_out), (b, b_out), (c, c_out), (d, d_out)))
    ]
    for one in moves:
        one.start()
    for one in moves:
        one.wait()


def solution(mesh):
    n, T = mesh.shape["ctx"], mesh.shape["tp"]

    def step(queries, keys, values, utterance, w_out, cotangent):
        F, columns = queries.shape
        H = columns // HS
        G = n // H
        D = w_out.shape[1]
        width = cotangent.shape[1]
        Q = H * F
        vm = pltpu.VMEM
        dma = pltpu.SemaphoreType.DMA
        shapes = [
            vm((F, columns), BF16), vm((F, columns), BF16), vm((F, columns), BF16),
            vm((1, F), jnp.int32), vm((columns, D), BF16),
            vm((T, F, width), BF16),
            vm((H, F + SLOTS, 2 * HS), BF16), vm((G, H, F + SLOTS, 2 * HS), BF16), vm((G, H, 2 * HS, F), BF16),
            vm((H, HS, F), BF16), vm((H, HS, F), BF16), vm((H, HS, F), BF16), vm((H, HS, F), BF16),
            vm((H, HS, F), BF16), vm((H, HS, F), BF16), vm((H, HS, F), BF16), vm((H, HS, F), BF16),
            vm((G, H, F, Q), F32), vm((G, 1, Q), F32),
            vm((G, H, F, 2 * HS), BF16), vm((G, H, F, 2 * HS), BF16),
            vm((H, F, 2 * HS), BF16), vm((H, F, 2 * HS), BF16),
            vm((T, F, width), BF16), vm((T, F, width), BF16),
            dma((6,)),
        ] + [dma((H,))] * 12 + [dma((G, H))] * 4 + [dma((T,))] * 4
        whole = pl.BlockSpec(memory_space=pltpu.HBM)
        here = pl.BlockSpec(memory_space=pltpu.VMEM)
        def pin(x):
            return pltpu.with_memory_space_constraint(x, pltpu.HBM)

        made = pl.pallas_call(
            functools.partial(kernel, (H, G, T, F)),
            out_shape=(
                jax.ShapeDtypeStruct((F, width), BF16),
                jax.ShapeDtypeStruct((F, columns), BF16),
                jax.ShapeDtypeStruct((F, columns), BF16),
                jax.ShapeDtypeStruct((F, columns), BF16),
            ),
            in_specs=[whole] * 6,
            out_specs=(here, here, here, here),
            scratch_shapes=shapes,
            compiler_params=pltpu.CompilerParams(
                collective_id=0, has_side_effects=True, vmem_limit_bytes=48 * 1024 * 1024
            ),
        )(pin(queries), pin(keys), pin(values), pin(utterance.reshape(1, F)), pin(w_out), pin(cotangent))
        return pl.pallas_call(
            store,
            out_shape=tuple(jax.ShapeDtypeStruct(x.shape, x.dtype) for x in made),
            in_specs=[here] * 4,
            out_specs=(whole,) * 4,
            scratch_shapes=[dma((4,))],
            compiler_params=pltpu.CompilerParams(vmem_limit_bytes=2 * 1024 * 1024),
        )(*made)

    placed = (P("ctx", "tp"), P("ctx", "tp"), P("ctx", "tp"), P("ctx"), P("tp", None), P("ctx", "tp"))
    return jax.shard_map(
        step, mesh=mesh, in_specs=placed, out_specs=(P("ctx", "tp"),) * 4, check_vma=False
    )
```

```python
import functools
import math

import jax
import jax.numpy as jnp
from jax import lax
from jax.experimental import pallas as pl
from jax.experimental.pallas import tpu as pltpu
from jax.sharding import PartitionSpec as P

HS = 64
SLOTS = 16
APART = 131072.0
MESH = pl.DeviceIdType.MESH
F32 = jnp.float32
BF16 = jnp.bfloat16


def loop(low, high, body, carry):
    if high - low <= 1:
        for i in range(low, high):
            carry = body(i, carry)
        return carry
    return lax.fori_loop(low, high, body, carry)


def pairs(items):
    items = list(items)
    step = 2 if len(items) % 2 == 0 else 1
    return [items[i:i + step] for i in range(0, len(items), step)]


def dot_nn(a, b):
    return jnp.dot(a, b, preferred_element_type=F32)


def dot_nt(a, b):
    return lax.dot_general(a, b, (((1,), (1,)), ((), ())), preferred_element_type=F32)


def turned(x):
    return jnp.transpose(x.astype(F32)).astype(BF16)


def remote(src, dst, send, recv, device):
    return pltpu.make_async_remote_copy(
        src_ref=src, dst_ref=dst, send_sem=send, recv_sem=recv, device_id=device, device_id_type=MESH
    )


def kernel(
    dims,
    q_in, k_in, v_in, u_in, w_in, c_in,
    out_ref, dq_ref, dk_ref, dv_ref,
    q_v, k_v, v_v, u_v, w_v, cot,
    kv_snd, kv_all, kv_turn, q_snd, q_rcv, do_snd, do_rcv, o_snd, o_rcv, dq_snd, dq_rcv,
    grid, tops, part_snd, part_rcv, fin_snd, fin_rcv, rs_snd, rs_rcv,
    local_sem, kv_s, kv_r, q_s, q_r, do_s, do_r, o_s, o_r, dq_s, dq_r, fin_s, fin_r,
    row_s, row_r, part_s, part_r, cot_s, cot_r, rs_s, rs_r,
):
    H, G, T, F = dims
    c = lax.axis_index("ctx")
    t = lax.axis_index("tp")
    h = c // G
    g = lax.rem(c, G)
    scale = HS ** (-0.5)
    expo = scale * math.log2(math.e)
    Q = H * F

    def up(d):
        return lax.rem(h + d, H)

    def side(e):
        return lax.rem(g + e, G)

    def lane(f):
        return lax.rem(t + f, T)

    barrier = pltpu.get_barrier_semaphore()

    def greet(device):
        pl.semaphore_signal(barrier, inc=1, device_id=device, device_id_type=MESH)

    for d in range(1, H):
        greet((up(d) * G + g, t))

    def greet_side(e, carry):
        greet((h * G + side(e), t))
        return carry

    loop(1, G, greet_side, 0)
    for f in range(1, T):
        greet((c, lane(f)))

    loads = [
        pltpu.make_async_copy(src, dst, local_sem.at[i])
        for i, (src, dst) in enumerate(
            ((k_in, k_v), (v_in, v_v), (q_in, q_v), (c_in, cot.at[t]), (w_in, w_v), (u_in, u_v))
        )
    ]
    for one in loads:
        one.start()

    loads[5].wait()
    same = (lax.broadcasted_iota(jnp.int32, (SLOTS, F), 0) == u_v[...]).astype(F32).astype(BF16)
    loads[0].wait()
    loads[1].wait()
    keys, values = k_v[...], v_v[...]
    for i in range(H):
        cols = slice(i * HS, (i + 1) * HS)
        kv_snd[i, 0:F, :] = jnp.concatenate([keys[:, cols], values[:, cols]], axis=1)
        kv_snd[i, F:, :] = same
    loads[2].wait()
    q_turn = turned(q_v[...])
    for i in range(H):
        q_snd[i] = q_turn[i * HS:(i + 1) * HS, :]
    loads[3].wait()
    pl.semaphore_wait(barrier, (H - 1) + (G - 1) + (T - 1))

    def kv_copy(to, at):
        return remote(kv_snd.at[to], kv_all.at[g, at], kv_s.at[to], kv_r.at[at], (to * G + g, t))

    def column(snd, rcv, send, recv):
        def build(to, at):
            return remote(snd.at[to], rcv.at[at], send.at[to], recv.at[at], (to * G + g, t))
        return build

    q_copy = column(q_snd, q_rcv, q_s, q_r)
    do_copy = column(do_snd, do_rcv, do_s, do_r)
    o_copy = column(o_snd, o_rcv, o_s, o_r)
    dq_copy = column(dq_snd, dq_rcv, dq_s, dq_r)
    fin_copy = column(fin_snd, fin_rcv, fin_s, fin_r)

    def row_copy(to, at, block):
        return remote(
            kv_all.at[at, block], kv_all.at[at, block], row_s.at[to, block], row_r.at[at, block],
            (h * G + to, t),
        )

    def part_copy(to, at, block):
        return remote(
            part_snd.at[to, block], part_rcv.at[at, block], part_s.at[to, block], part_r.at[at, block],
            (h * G + to, t),
        )

    def cot_copy(to, at, turn):
        return remote(cot.at[at], cot.at[at], cot_s.at[turn], cot_r.at[at], (c, to))

    def rs_copy(to, at):
        return remote(rs_snd.at[to], rs_rcv.at[at], rs_s.at[to], rs_r.at[at], (c, to))

    def send_column(build):
        for d in range(1, H):
            build(up(d), h).start()

    def wait_column(build):
        for d in range(H - 1, 0, -1):
            build(up(d), up(d)).wait_recv()

    def sent_column(build):
        for d in range(1, H):
            build(up(d), h).wait_send()

    partner = t + 1 - 2 * lax.rem(t, 2)
    for f in range(2, T, 2):
        cot_copy(lane(f), t, f).start()
    cot_copy(partner, t, 0).start()
    for d in range(1, H):
        kv_copy(up(d), h).start()
        q_copy(up(d), h).start()
    kv_all[g, h] = kv_snd[h]
    q_rcv[h] = q_snd[h]

    def forward(block):
        def step(e, carry):
            row_copy(side(e), g, block).start()
            return carry
        loop(1, G, step, 0)

    forward(h)
    for d in range(H - 1, 0, -1):
        kv_copy(up(d), up(d)).wait_recv()
        forward(up(d))
        if d == H - 1:
            for f in range(2, T, 2):
                cot_copy(lane(f), lane(f), f).wait_recv()
                cot_copy(partner, lane(f), f + 1).start()

    loads[4].wait()
    for f in range(0, T, 2):
        at = lax.rem(partner + f, T)
        cot_copy(partner, at, f).wait_recv()
    width = cot.shape[2]
    grad = dot_nt(w_v[:, 0:width], cot[0])
    for i in range(1, T):
        grad += dot_nt(w_v[:, i * width:(i + 1) * width], cot[i])
    grad = grad.astype(BF16)
    for i in range(H):
        do_snd[i] = grad[i * HS:(i + 1) * HS, :]
    send_column(do_copy)
    do_rcv[h] = do_snd[h]

    wait_column(q_copy)
    q_all = jnp.concatenate([q_rcv[i] for i in range(H)], axis=1)

    def away(i):
        hot = kv_all[g, i, F:, :].astype(F32)
        return ((hot - 1.0) * APART).astype(BF16)

    q_wide = jnp.concatenate([q_all, jnp.concatenate([away(i) for i in range(H)], axis=1)], axis=0)

    def ahead(at):
        top = None
        for i in range(H):
            block = kv_all[at, i, 0:F, :]
            kv_turn[at, i] = turned(block)
            hot = turned(kv_all[at, i, F:, :])
            wide = jnp.concatenate([block[:, 0:HS], hot], axis=1)
            s = dot_nn(wide, q_wide)
            grid[at, i] = s
            here = jnp.max(s, axis=0, keepdims=True)
            top = here if top is None else jnp.maximum(top, here)
        tops[at] = top
        total, mixed = jnp.zeros((1, Q), F32), jnp.zeros((HS, Q), F32)
        for pair in pairs(range(H)):
            parts = []
            for i in pair:
                w = jnp.exp2((grid[at, i] - top) * expo)
                grid[at, i] = w
                total = total + jnp.sum(w, axis=0, keepdims=True)
                parts.append(w.astype(BF16))
            lanes = jnp.concatenate([kv_turn[at, i, HS:, :] for i in pair], axis=1)
            mixed = mixed + dot_nn(lanes, jnp.concatenate(parts, axis=0))
        return top, total, mixed

    def ahead_side(e, carry):
        top, total, mixed = carry
        at = side(e)
        for i in range(H):
            row_copy(at, at, i).wait_recv()
        new, more, other = ahead(at)
        both = jnp.maximum(top, new)
        old_part, new_part = jnp.exp2((top - both) * expo), jnp.exp2((new - both) * expo)
        return both, total * old_part + more * new_part, mixed * old_part + other * new_part

    top, total, mixed = loop(1, G, ahead_side, ahead(g))
    inverse = 1.0 / total
    attn = (mixed * inverse).astype(BF16)
    for i in range(H):
        o_snd[i] = attn[:, i * F:(i + 1) * F]
    send_column(o_copy)
    o_rcv[h] = o_snd[h]

    wait_column(do_copy)
    do_all = jnp.concatenate([do_rcv[i] for i in range(H)], axis=1)
    delta = jnp.sum(do_all.astype(F32) * attn.astype(F32), axis=0, keepdims=True)

    def back(at, pair):
        factor = jnp.exp2((tops[at] - top) * expo) * inverse
        p = jnp.concatenate([grid[at, b] for b in pair], axis=0) * factor
        dv = dot_nt(p.astype(BF16), do_all)
        rows = jnp.concatenate([kv_all[at, b, 0:F, HS:] for b in pair], axis=0)
        ds = (p * (dot_nn(rows, do_all) - delta)).astype(BF16)
        dk = dot_nt(ds, q_all) * scale
        dq = dot_nn(jnp.concatenate([kv_turn[at, b, 0:HS, :] for b in pair], axis=1), ds)
        return jnp.concatenate([dk, dv], axis=1), dq

    order = [up(d) for d in range(1, H)] + [h]

    def back_side(e, query_total):
        at = side(e)
        for pair in pairs(order):
            part, dq = back(at, pair)
            for i, b in enumerate(pair):
                part_snd[at, b] = part[i * F:(i + 1) * F, :].astype(BF16)
                part_copy(at, g, b).start()
            query_total = query_total + dq
        return query_total

    query_total = loop(1, G, back_side, jnp.zeros((HS, Q), F32))

    def project():
        wait_column(o_copy)
        mine = turned(jnp.concatenate([o_rcv[i] for i in range(H)], axis=0))
        for i in range(T):
            rs_snd[i] = dot_nn(mine, w_v[:, i * width:(i + 1) * width]).astype(BF16)
        for f in range(1, T):
            rs_copy(lane(f), t).start()
        rs_rcv[t] = rs_snd[t]

    def finish(b, part):
        def gather(e, sofar):
            at = side(e)
            part_copy(at, at, b).wait_recv()
            return sofar + part_rcv[at, b].astype(F32)

        fin_snd[b] = loop(1, G, gather, part).astype(BF16)

    for number, pair in enumerate(pairs(order)):
        part, dq = back(g, pair)
        query_total = query_total + dq
        for i, b in enumerate(pair):
            finish(b, part[i * F:(i + 1) * F, :])
            if number * len(pair) + i < H - 1:
                fin_copy(b, h).start()
        if number == 0:
            project()
    fin_rcv[h] = fin_snd[h]
    query_out = (query_total * scale).astype(BF16)
    for i in range(H):
        dq_snd[i] = query_out[:, i * F:(i + 1) * F]
    send_column(dq_copy)
    dq_rcv[h] = dq_snd[h]

    for f in range(1, T):
        rs_copy(lane(f), lane(f)).wait_recv()
    summed = rs_rcv[0].astype(F32)
    for i in range(1, T):
        summed += rs_rcv[i].astype(F32)
    out_ref[...] = summed.astype(BF16)

    wait_column(dq_copy)
    dq_ref[...] = turned(jnp.concatenate([dq_rcv[i] for i in range(H)], axis=0))
    wait_column(fin_copy)
    dk_ref[...] = jnp.concatenate([fin_rcv[i, :, 0:HS] for i in range(H)], axis=1)
    dv_ref[...] = jnp.concatenate([fin_rcv[i, :, HS:] for i in range(H)], axis=1)

    for build in (kv_copy, q_copy, do_copy, o_copy, dq_copy, fin_copy):
        sent_column(build)

    def sent_side(e, carry):
        for i in range(H):
            row_copy(side(e), g, i).wait_send()
            part_copy(side(e), g, i).wait_send()
        return carry

    loop(1, G, sent_side, 0)
    for f in range(1, T):
        rs_copy(lane(f), t).wait_send()
    cot_copy(partner, t, 0).wait_send()
    for f in range(2, T, 2):
        cot_copy(lane(f), t, f).wait_send()
        cot_copy(partner, lane(f), f + 1).wait_send()


def store(a, b, c, d, a_out, b_out, c_out, d_out, sem):
    moves = [
        pltpu.make_async_copy(src, dst, sem.at[i])
        for i, (src, dst) in enumerate(((a, a_out), (b, b_out), (c, c_out), (d, d_out)))
    ]
    for one in moves:
        one.start()
    for one in moves:
        one.wait()


def solution(mesh):
    n, T = mesh.shape["ctx"], mesh.shape["tp"]

    def step(queries, keys, values, utterance, w_out, cotangent):
        F, columns = queries.shape
        H = columns // HS
        G = n // H
        D = w_out.shape[1]
        width = cotangent.shape[1]
        Q = H * F
        vm = pltpu.VMEM
        dma = pltpu.SemaphoreType.DMA
        shapes = [
            vm((F, columns), BF16), vm((F, columns), BF16), vm((F, columns), BF16),
            vm((1, F), jnp.int32), vm((columns, D), BF16),
            vm((T, F, width), BF16),
            vm((H, F + SLOTS, 2 * HS), BF16), vm((G, H, F + SLOTS, 2 * HS), BF16), vm((G, H, 2 * HS, F), BF16),
            vm((H, HS, F), BF16), vm((H, HS, F), BF16), vm((H, HS, F), BF16), vm((H, HS, F), BF16),
            vm((H, HS, F), BF16), vm((H, HS, F), BF16), vm((H, HS, F), BF16), vm((H, HS, F), BF16),
            vm((G, H, F, Q), F32), vm((G, 1, Q), F32),
            vm((G, H, F, 2 * HS), BF16), vm((G, H, F, 2 * HS), BF16),
            vm((H, F, 2 * HS), BF16), vm((H, F, 2 * HS), BF16),
            vm((T, F, width), BF16), vm((T, F, width), BF16),
            dma((6,)),
        ] + [dma((H,))] * 12 + [dma((G, H))] * 4 + [dma((T,))] * 4
        whole = pl.BlockSpec(memory_space=pltpu.HBM)
        here = pl.BlockSpec(memory_space=pltpu.VMEM)
        def pin(x):
            return pltpu.with_memory_space_constraint(x, pltpu.HBM)

        made = pl.pallas_call(
            functools.partial(kernel, (H, G, T, F)),
            out_shape=(
                jax.ShapeDtypeStruct((F, width), BF16),
                jax.ShapeDtypeStruct((F, columns), BF16),
                jax.ShapeDtypeStruct((F, columns), BF16),
                jax.ShapeDtypeStruct((F, columns), BF16),
            ),
            in_specs=[whole] * 6,
            out_specs=(here, here, here, here),
            scratch_shapes=shapes,
            compiler_params=pltpu.CompilerParams(
                collective_id=0, has_side_effects=True, vmem_limit_bytes=48 * 1024 * 1024
            ),
        )(pin(queries), pin(keys), pin(values), pin(utterance.reshape(1, F)), pin(w_out), pin(cotangent))
        return pl.pallas_call(
            store,
            out_shape=tuple(jax.ShapeDtypeStruct(x.shape, x.dtype) for x in made),
            in_specs=[here] * 4,
            out_specs=(whole,) * 4,
            scratch_shapes=[dma((4,))],
            compiler_params=pltpu.CompilerParams(vmem_limit_bytes=2 * 1024 * 1024),
        )(*made)

    placed = (P("ctx", "tp"), P("ctx", "tp"), P("ctx", "tp"), P("ctx"), P("tp", None), P("ctx", "tp"))
    return jax.shard_map(
        step, mesh=mesh, in_specs=placed, out_specs=(P("ctx", "tp"),) * 4, check_vma=False
    )
```
